32 devices in a mesh: tensor: 4 (over z), tokens: 8 (over y, x, core).
Axes of the slice: x: 2, y: 2, z: 4, core: 2. Of those that a mesh axis runs over, the one named last changes fastest.
Arguments:
- hidden: bfloat16 [2048, 8192], P('tokens', 'tensor'), may hold values from -24 to 24
- w_query: bfloat16 [8192, 4096], P(None, 'tensor'), may hold values from -0.0625 to 0.0625
- w_key: bfloat16 [8192, 512], P(None, 'tensor'), may hold values from -0.0625 to 0.0625
- w_value: bfloat16 [8192, 512], P(None, 'tensor'), may hold values from -0.0625 to 0.0625
- key_codes: int32 [2048, 512], P('tokens', 'tensor'), may hold values from 0 to 15
- codebook: float32 [512, 16], P('tensor'), may hold values from -24 to 24
- positions: int32 [2048], P('tokens'), may hold values from 0 to 1535, as said below
- cotangent: bfloat16 [2048, 4096], P('tokens', 'tensor'), may hold values from -6 to 6
Outputs:
- attention_out: bfloat16 [2048, 4096], P('tokens', 'tensor')
- codebook_grad: float32 [512, 16], P('tensor')
The draws below stay inside these ranges and needn't reach their ends.
Inputs may be any that keep to these rules, and one draw needn't show every extreme that they name: positions are 0 at the first token of each packed document and rise by one within it; exactly one document has 1536 tokens and every other is shorter.
All inputs are finite; a program needn't handle non-finite values.
Results may differ from the reference program's by a relative error of at most 0.0095.
The reference program's roundings to bfloat16 on the way count: a program that leaves them out, or rounds other values in their place, can miss the bound.
Values may be sent and summed in bfloat16 or wider, within the bound.
A program may use at most 128 MiB of HBM per device.

```python
import math
import jax
import jax.numpy as jnp
from jax import lax

D = 8192
HD = 128
LEVELS = 16
QH = 32
KVH = 4
SEQ = 2048


def draw_hidden(key, part):
    base = jnp.clip(jax.random.normal(jax.random.fold_in(key, 11), (SEQ, D), jnp.float32), -4.0, 4.0)
    shared = jax.random.normal(jax.random.fold_in(key, 13), (1, D), jnp.float32)
    lower, upper = (math.log(0.5), math.log(2.0))
    shared = jnp.clip(shared, -3.0, 3.0)
    row_scale = jnp.exp(jax.random.uniform(jax.random.fold_in(key, 12), (SEQ, 1), jnp.float32, lower, upper))
    return (base * row_scale + shared).astype(jnp.bfloat16)


def draw_codebook(key, part):
    base = jnp.clip(jax.random.normal(jax.random.fold_in(key, 21), (KVH * HD, LEVELS), jnp.float32), -4.0, 4.0)
    lower, upper = (math.log(0.5), math.log(2.0))
    channel_scale = jnp.exp(jax.random.uniform(jax.random.fold_in(key, 22), (KVH * HD, 1), jnp.float32, lower, upper))
    return base * channel_scale


def draw_positions(key, part):
    longest = 3 * SEQ // 4
    first = jax.random.randint(jax.random.fold_in(key, 31), (), 0, SEQ - longest + 1)
    index = jnp.arange(SEQ).astype(jnp.int32)
    spacing = max(4, SEQ // 32)
    marks = jax.random.randint(jax.random.fold_in(key, 32), (SEQ,), 0, spacing) == 0
    inside = (index > first) & (index < first + longest)
    marks = marks & jnp.logical_not(inside) | (index == 0) | (index == first) | (index == first + longest)
    starts = lax.cummax(jnp.where(marks, index, 0), axis=0)
    return (index - starts).astype(jnp.int32)


def with_ends(values, own_key, smallest, largest):
    place = [jax.random.randint(jax.random.fold_in(own_key, axis), (), 0, length) for axis, length in enumerate(values.shape)]
    widest = values.shape.index(max(values.shape))
    neighbour = place[:widest] + [(place[widest] + 1) % values.shape[widest]] + place[widest + 1:]
    return values.at[tuple(place)].set(smallest).at[tuple(neighbour)].set(largest)


def block_levels(key, shape, cuts, smallest, high):
    factor_of, own = 1.0, jax.random.fold_in(key, 6)
    for axis_at, shards_of in cuts:
        heights = jnp.exp(jax.random.uniform(jax.random.fold_in(own, axis_at), (shards_of,), jnp.float32, smallest / len(cuts), high / len(cuts)))
        factor_of = factor_of * jnp.repeat(heights, shape[axis_at] // shards_of).reshape([-1 if axis == axis_at else 1 for axis in range(len(shape))])
    return factor_of


def centred(own_key, dims, deviation, reach, split=(), kind=jnp.bfloat16):
    array = jax.random.normal(own_key, dims, jnp.float32) * deviation
    if len(split) > 0:
        array = block_levels(own_key, dims, split, -0.22, 0.18) * array
    return jnp.clip(array, min=-reach, max=reach).astype(kind)


def setup_inputs(seed: int = 0) -> dict:
    key_of = jax.random.split(jax.random.key(seed), 9)
    return {
        "hidden": draw_hidden(jax.random.fold_in(key_of[8], 71), 0),
        "w_query": centred(key_of[1], (D, QH * HD), D ** -0.5, 0.0625, ((1, 4),)),
        "w_key": centred(key_of[2], (D, KVH * HD), D ** -0.5, 0.0625, ((1, 4),)),
        "w_value": centred(key_of[3], (D, KVH * HD), D ** -0.5, 0.0625, ((1, 4),)),
        "key_codes": with_ends(jax.random.randint(key_of[4], (SEQ, KVH * HD), 0, LEVELS), jax.random.fold_in(key_of[4], 1), 0, LEVELS - 1).astype(jnp.int32),
        "codebook": draw_codebook(jax.random.fold_in(key_of[8], 71), 0),
        "positions": draw_positions(jax.random.fold_in(key_of[8], 71), 0),
        "cotangent": centred(key_of[7], (SEQ, QH * HD), 1.0, 6.0, ((0, 8), (1, 4))),
    }


ROPE_BASE = 500000.0
NEG_BIG = -1e+30

def rope_tables(positions, width):
    index = jnp.arange(width // 2).astype(jnp.float32)
    inverse = jnp.exp(index * (-2.0 * math.log(ROPE_BASE) / width))
    angle = positions.astype(jnp.float32)[:, None] * inverse[None, :]
    return (jnp.cos(angle), jnp.sin(angle))

def rotate(values, cosine, sine):
    half = values.shape[-1] // 2
    first = values[..., :half]
    second = values[..., half:]
    return jnp.concatenate([first * cosine - second * sine, second * cosine + first * sine], axis=-1)

def unrotate(grads, cosine, sine):
    half = grads.shape[-1] // 2
    first = grads[..., :half]
    second = grads[..., half:]
    return jnp.concatenate([first * cosine + second * sine, second * cosine - first * sine], axis=-1)

def reference(hidden, w_query, w_key, w_value, key_codes, codebook, positions, cotangent):
    query_pre = jnp.dot(hidden, w_query, preferred_element_type=jnp.float32)
    key_true = jnp.dot(hidden, w_key, preferred_element_type=jnp.float32)
    value_all = jnp.dot(hidden, w_value, preferred_element_type=jnp.float32).astype(jnp.bfloat16)
    channels = jnp.arange(KVH * HD).astype(jnp.int32)
    key_deq = codebook[channels[None, :], key_codes]
    cosine, sine = rope_tables(positions, HD)
    query_rot = rotate(query_pre.reshape(SEQ, QH, HD).transpose(1, 0, 2), cosine, sine).astype(jnp.bfloat16)
    key_rot = rotate(key_deq.reshape(SEQ, KVH, HD).transpose(1, 0, 2), cosine, sine).astype(jnp.bfloat16)
    values = value_all.reshape(SEQ, KVH, HD).transpose(1, 0, 2)
    cot = cotangent.reshape(SEQ, QH, HD).transpose(1, 0, 2)
    index = jnp.arange(SEQ).astype(jnp.int32)
    spacing = index[:, None] - index[None, :]
    visible = (spacing >= 0) & (spacing <= positions[:, None])
    scale = 1.0 / math.sqrt(HD)
    group = QH // KVH

    def one_head(head):
        kv_head = head // group
        query = query_rot[head]
        keys = key_rot[kv_head]
        vals = values[kv_head]
        grad_out = cot[head]
        scores = jnp.dot(query, keys.T, preferred_element_type=jnp.float32) * scale
        masked = jnp.where(visible, scores, NEG_BIG)
        peak = lax.optimization_barrier(jnp.max(masked, axis=1))
        mass = lax.optimization_barrier(jnp.sum(jnp.where(visible, jnp.exp(masked - peak[:, None]), 0.0), axis=1))
        log_total = peak + jnp.log(mass)
        probs = jnp.where(visible, jnp.exp(masked - log_total[:, None]), 0.0)
        output = jnp.dot(probs.astype(jnp.bfloat16), vals, preferred_element_type=jnp.float32).astype(jnp.bfloat16)
        delta = lax.optimization_barrier(jnp.sum(grad_out.astype(jnp.float32) * output.astype(jnp.float32), axis=1))
        dprobs = jnp.dot(grad_out, vals.T, preferred_element_type=jnp.float32)
        dscores = (probs * (dprobs - delta[:, None])).astype(jnp.bfloat16)
        dkey = jnp.dot(dscores.T, query, preferred_element_type=jnp.float32) * scale
        return (output, dkey)
    outputs, dkeys = lax.map(one_head, jnp.arange(QH).astype(jnp.int32))
    attention_out = outputs.transpose(1, 0, 2).reshape(SEQ, QH * HD)
    key_grad_rot = lax.optimization_barrier(jnp.sum(dkeys.reshape(KVH, group, SEQ, HD), axis=1))
    key_grad_pre = unrotate(key_grad_rot, cosine, sine).transpose(1, 0, 2).reshape(SEQ, KVH * HD)
    entry_grad = key_grad_pre + LEVELS / SEQ * (key_deq - key_true)
    codebook_grad = jnp.zeros((KVH * HD, LEVELS), jnp.float32).at[jnp.broadcast_to(channels[None, :], key_codes.shape), key_codes].add(entry_grad)
    return (attention_out, codebook_grad)
```

```python
import functools
import math

import jax
import jax.numpy as jnp
from jax import lax
from jax.experimental import pallas as pl
from jax.experimental.pallas import tpu as pltpu
from jax.sharding import PartitionSpec as P

HD = 128
ROPE_BASE = 500000.0
NEG_BIG = -1e30
SUBS = 4
MESH = pl.DeviceIdType.MESH


def trig_table(positions, width):
    index = jnp.arange(width // 2).astype(jnp.float32)
    inverse = jnp.exp(index * (-2.0 * math.log(ROPE_BASE) / width))
    angle = positions.astype(jnp.float32)[:, None] * jnp.tile(inverse, 2)[None, :]
    low = jnp.arange(width) < width // 2
    return jnp.where(low[None, :], jnp.cos(angle), jnp.sin(angle))


def split_trig(table):
    low = lax.broadcasted_iota(jnp.int32, table.shape, 1) < HD // 2
    rolled = pltpu.roll(table, HD // 2, 1)
    return jnp.where(low, table, rolled), jnp.where(low, -rolled, table)


def dot_nt(a, b):
    return lax.dot_general(a, b, (((1,), (1,)), ((), ())), preferred_element_type=jnp.float32)


def kernel(
    n_t, n_d, heads,
    x_hbm, wq_hbm, wk_hbm, wv_hbm, codes_hbm, trig_hbm, cbt, pos, cot,
    out_ref, grad_ref,
    xbuf, w, acc, codes, trig, kall, vall, vt, qst, dost, dot_t, probs, scores, deltas, bins, red, poss, outs,
    xsend, xrecv, xlocal, wsem, csend, crecv, clocal, ksend, krecv, vsend, vrecv, rsend, rrecv,
):
    subs, tile, feats = x_hbm.shape
    cols = heads * tile
    rows = subs * tile
    total = rows * n_d
    levels = cbt.shape[0]
    qw = heads * HD
    width = qw + 2 * HD
    scale = 1.0 / math.sqrt(HD)
    longest = 3 * total // 4
    z = lax.axis_index("tensor")
    d = lax.axis_index("tokens")
    has_left, has_right = z > 0, z < n_t - 1
    first = jnp.maximum(d - longest // rows, 0)
    last = d + 1

    barrier = pltpu.get_barrier_semaphore()

    @pl.when(has_left)
    def _():
        pl.semaphore_signal(barrier, inc=1, device_id={"tensor": z - 1}, device_id_type=MESH)

    @pl.when(has_right)
    def _():
        pl.semaphore_signal(barrier, inc=1, device_id={"tensor": z + 1}, device_id_type=MESH)

    for k in range(1, n_d):
        pl.semaphore_signal(
            barrier, inc=1, device_id={"tokens": lax.rem(d + k, n_d)}, device_id_type=MESH
        )

    def block(src):
        return pl.ds(pl.multiple_of(src * feats, feats), feats)

    def w_copies(src):
        return [
            pltpu.make_async_copy(wq_hbm.at[block(src)], w.at[block(src), pl.ds(0, qw)], wsem.at[0, src]),
            pltpu.make_async_copy(wk_hbm.at[block(src)], w.at[block(src), pl.ds(qw, HD)], wsem.at[1, src]),
            pltpu.make_async_copy(wv_hbm.at[block(src)], w.at[block(src), pl.ds(qw + HD, HD)], wsem.at[2, src]),
        ]

    x_own = pltpu.make_async_copy(x_hbm, xbuf.at[:, z], xlocal)
    c_own = pltpu.make_async_copy(codes_hbm, codes.at[d], clocal.at[0])
    t_own = pltpu.make_async_copy(trig_hbm, trig.at[d], clocal.at[1])
    c_own.start()
    t_own.start()
    x_own.start()
    for k in range(n_t):
        for copy in w_copies(lax.rem(z + k, n_t)):
            copy.start()

    pl.semaphore_wait(
        barrier, n_d - 1 + has_left.astype(jnp.int32) + has_right.astype(jnp.int32)
    )

    def own_hop(s, side):
        return pltpu.make_async_remote_copy(
            src_ref=x_hbm.at[s], dst_ref=xbuf.at[s, z],
            send_sem=xsend.at[side, s, z], recv_sem=xrecv.at[s, z],
            device_id={"tensor": z + 2 * side - 1}, device_id_type=MESH,
        )

    def hop(s, src, side):
        return pltpu.make_async_remote_copy(
            src_ref=xbuf.at[s, src], dst_ref=xbuf.at[s, src],
            send_sem=xsend.at[side, s, src], recv_sem=xrecv.at[s, src],
            device_id={"tensor": z + 2 * side - 1}, device_id_type=MESH,
        )

    for s in range(subs):
        @pl.when(has_right)
        def _():
            own_hop(s, 1).start()

        @pl.when(has_left)
        def _():
            own_hop(s, 0).start()

    def take(s, k):
        @pl.when(z - k >= 0)
        def _():
            hop(s, z - k, 1).wait_recv()

        @pl.when(z + k < n_t)
        def _():
            hop(s, z + k, 0).wait_recv()

    def forward(s, k):
        @pl.when((z - k >= 0) & has_right)
        def _():
            hop(s, z - k, 1).start()

        @pl.when((z + k < n_t) & has_left)
        def _():
            hop(s, z + k, 0).start()

    def key_copies(k):
        peer = {"tokens": lax.rem(d + k, n_d)}
        return [
            pltpu.make_async_remote_copy(
                src_ref=codes_hbm, dst_ref=codes.at[d],
                send_sem=csend.at[0, k], recv_sem=crecv.at[0, k],
                device_id=peer, device_id_type=MESH,
            ),
            pltpu.make_async_remote_copy(
                src_ref=trig_hbm, dst_ref=trig.at[d],
                send_sem=csend.at[1, k], recv_sem=crecv.at[1, k],
                device_id=peer, device_id_type=MESH,
            ),
        ]

    def dequantize(code):
        value = jnp.zeros(code.shape, jnp.float32)
        for level in range(levels):
            value = jnp.where(code == level, cbt[level:level + 1, :], value)
        return value

    def sub_rows(s):
        return pl.ds(pl.multiple_of(s * tile, tile), tile)

    c_own.wait()
    t_own.wait()
    for s in range(subs):
        mine = pl.ds(s * tile, tile)
        cosine, sine = split_trig(trig[d, mine])
        value = dequantize(codes[d, mine])
        turned = value * cosine + pltpu.roll(value, HD // 2, 1) * sine
        kall[d, mine] = turned.astype(jnp.bfloat16)

    def rot_copy(k):
        return pltpu.make_async_remote_copy(
            src_ref=kall.at[d], dst_ref=kall.at[d],
            send_sem=ksend.at[k], recv_sem=krecv.at[k],
            device_id={"tokens": lax.rem(d + k, n_d)}, device_id_type=MESH,
        )

    for k in range(1, n_d):
        rot_copy(k).start()
    for k in range(1, n_d):
        for copy in key_copies(k):
            copy.start()

    lane = lax.broadcasted_iota(jnp.int32, (8, HD), 1)
    for s in range(subs):
        at = s * tile // HD * HD
        here = jnp.broadcast_to(pos[:, at:at + HD], (8, HD))
        start = s * tile % HD
        spread = here
        for piece in range(HD // tile):
            shift = (piece * tile - start) % HD
            moved = pltpu.roll(here, shift, 1) if shift else here
            spread = jnp.where(lane // tile == piece, moved, spread)
        poss[s] = spread
    bins[...] = jnp.zeros_like(bins)
    outs[...] = jnp.zeros_like(outs)
    acc[...] = jnp.zeros_like(acc)

    for s in range(subs):
        for h in range(heads):
            piece = cot[s * tile:(s + 1) * tile, h * HD:(h + 1) * HD]
            dost[s, h * tile:(h + 1) * tile, :] = piece
        dot_t[s] = dost[s].astype(jnp.float32).T

    def clear(b, carry):
        @pl.when((b < first) | (b >= last))
        def _():
            for s in range(subs):
                probs[s, b] = jnp.zeros((rows, cols), jnp.bfloat16)

        return carry

    lax.fori_loop(0, n_d, clear, 0)

    def add_bins(code, value):
        for level in range(levels):
            chosen = jnp.where(code == level, value, 0.0)
            bins[level] += jnp.sum(chosen.reshape(-1, 8, HD), axis=0)

    def v_copy(s, k):
        mine = vall.at[d, sub_rows(s)]
        return pltpu.make_async_remote_copy(
            src_ref=mine, dst_ref=mine,
            send_sem=vsend.at[s, k], recv_sem=vrecv.at[s, k],
            device_id={"tokens": lax.rem(d + k, n_d)}, device_id_type=MESH,
        )

    def take_values(c):
        for k in range(1, n_d):
            v_copy(c, k).wait_recv()
        part = vall[:, sub_rows(c), :].reshape(n_d * tile, HD)
        vt[c] = part.astype(jnp.float32).T.astype(jnp.bfloat16)

    def add_out(s, c):
        part = probs[s, :, sub_rows(c), :].reshape(n_d * tile, cols)
        outs[s] += jnp.dot(vt[c], part, preferred_element_type=jnp.float32)

    nw = 256 if width % 256 == 0 else HD

    def multiply_all(src):
        def columns(n, carry):
            at = pl.ds(pl.multiple_of(n * nw, nw), nw)
            acc[:, at] += jnp.dot(
                xbuf[:, src].reshape(rows, feats), w[block(src), at],
                preferred_element_type=jnp.float32,
            )
            return carry

        lax.fori_loop(0, width // nw, columns, 0)

    def multiply(s, src):
        acc[sub_rows(s), :] += jnp.dot(
            xbuf[s, src], w[block(src), :], preferred_element_type=jnp.float32
        )

    x_own.wait()

    def near(j, carry):
        src = z + lax.rem(j + 1, 3) - 1

        @pl.when((src >= 0) & (src < n_t))
        def _():
            for copy in w_copies(src):
                copy.wait()

            @pl.when(j == 1)
            def _():
                for s in range(1, subs):
                    hop(s, src, 1).wait_recv()

            @pl.when(j == 2)
            def _():
                for s in range(1, subs):
                    hop(s, src, 0).wait_recv()

            multiply_all(src)

        @pl.when(j == 0)
        def _():
            take(0, 1)
            forward(0, 1)

        return carry

    lax.fori_loop(0, 3, near, 0)
    for k in range(2, n_t):
        for src in (z - k, z + k):
            @pl.when((src >= 0) & (src < n_t))
            def _():
                for copy in w_copies(src):
                    copy.wait()

    def sub(s, carry):
        def step(k, inner):
            take(s, k)
            forward(s, k)

            @pl.when((k == 2) & (s + 1 < subs))
            def _():
                forward(s + 1, 1)

            def side(j, most):
                src = z + k * (2 * j - 1)

                @pl.when((src >= 0) & (src < n_t))
                def _():
                    multiply(s, src)

                return most

            return lax.fori_loop(0, 2, side, inner)

        lax.fori_loop(2, n_t, step, 0)
        mine = sub_rows(s)
        vall[d, mine, :] = acc[mine, qw + HD:qw + 2 * HD].astype(jnp.bfloat16)

        @pl.when(s == 0)
        def _():
            for k in range(1, n_d):
                rot_copy(k).wait_recv()

        for k in range(1, n_d):
            v_copy(s, k).start()
        cosine, sine = split_trig(trig[d, mine])
        for h in range(heads):
            value = acc[mine, h * HD:(h + 1) * HD]
            turned = value * cosine + pltpu.roll(value, HD // 2, 1) * sine
            qst[s, h * tile:(h + 1) * tile, :] = turned.astype(jnp.bfloat16)
        code = codes[d, mine]
        add_bins(code, (levels / total) * (dequantize(code) - acc[mine, qw:qw + HD]))

        column = lax.broadcasted_iota(jnp.int32, (1, HD), 1)
        query = d * rows + s * tile + (column & (tile - 1))
        earliest = query - poss[s, 0:1, :]
        q = qst[s]

        def score(b, peak):
            key = b * rows + lax.broadcasted_iota(jnp.int32, (rows, 1), 0)
            seen = (key <= query) & (key >= earliest)
            value = dot_nt(kall[b], q)
            tops = []
            for g in range(cols // HD):
                at = slice(g * HD, (g + 1) * HD)
                part = jnp.where(seen, value[:, at], NEG_BIG)
                scores[b, :, at] = part
                tops.append(jnp.max(part.reshape(-1, 8, HD), axis=0))
            return jnp.maximum(peak, jnp.concatenate(tops, axis=1))

        peak = lax.fori_loop(first, last, score, jnp.full((8, cols), NEG_BIG, jnp.float32))
        peak = jnp.max(peak, axis=0, keepdims=True)

        def exponent(b, mass):
            value = jnp.exp2((scores[b] - peak) * (scale * math.log2(math.e)))
            scores[b] = value
            return mass + jnp.sum(value.reshape(-1, 8, cols), axis=0)

        mass = lax.fori_loop(first, last, exponent, jnp.zeros((8, cols), jnp.float32))
        inverse = 1.0 / jnp.sum(mass, axis=0, keepdims=True)

        def normal(b, inner):
            probs[s, b] = (scores[b] * inverse).astype(jnp.bfloat16)
            return inner

        lax.fori_loop(first, last, normal, 0)

        @pl.when(s > 0)
        def _():
            take_values(s - 1)

            def older(c, inner):
                add_out(s, c)
                return inner

            def newest(q_at, inner):
                add_out(q_at, s - 1)
                return inner

            lax.fori_loop(0, s, older, 0)
            lax.fori_loop(0, s, newest, 0)

        return carry

    lax.fori_loop(0, subs, sub, 0)
    take_values(subs - 1)

    def close(s, carry):
        add_out(s, subs - 1)
        output = outs[s].astype(jnp.bfloat16).astype(jnp.float32)
        deltas[s] = jnp.broadcast_to(jnp.sum(output * dot_t[s], axis=0, keepdims=True), (8, cols))
        output = output.T.astype(jnp.bfloat16)
        for h in range(heads):
            out_ref[sub_rows(s), h * HD:(h + 1) * HD] = output[h * tile:(h + 1) * tile, :]
        return carry

    lax.fori_loop(0, subs, close, 0)
    for k in range(1, n_d):
        for copy in key_copies(k):
            copy.wait_recv()

    def backward(b, carry):
        grad = jnp.zeros((rows, HD), jnp.float32)
        values = vall[b]
        for s in range(subs):
            dprobs = dot_nt(values, dost[s])
            dscores = (probs[s, b].astype(jnp.float32) * (dprobs - deltas[s, 0:1, :])).astype(jnp.bfloat16)
            grad += jnp.dot(dscores, qst[s], preferred_element_type=jnp.float32)
        grad = grad * scale
        cosine, sine = split_trig(trig[b])
        add_bins(codes[b], grad * cosine - pltpu.roll(grad, HD // 2, 1) * sine)
        return carry

    lax.fori_loop(first, last, backward, 0)
    red[d] = jnp.sum(bins[...], axis=1)

    sums = [
        pltpu.make_async_remote_copy(
            src_ref=red.at[d], dst_ref=red.at[d],
            send_sem=rsend.at[k], recv_sem=rrecv.at[k],
            device_id={"tokens": lax.rem(d + k, n_d)}, device_id_type=MESH,
        )
        for k in range(1, n_d)
    ]
    for copy in sums:
        copy.start()

    def x_drain(s, carry):
        def one(src, inner):
            @pl.when(has_right & (src <= z))
            def _():
                hop(s, src, 1).wait_send()

            @pl.when(has_left & (src >= z))
            def _():
                hop(s, src, 0).wait_send()

            return inner

        lax.fori_loop(0, n_t, one, 0)
        for k in range(1, n_d):
            v_copy(s, k).wait_send()
        return carry

    lax.fori_loop(0, subs, x_drain, 0)
    for k in range(1, n_d):
        rot_copy(k).wait_send()
        for copy in key_copies(k):
            copy.wait_send()
    for copy in sums:
        copy.wait()
    grad_ref[...] = jnp.sum(red[...], axis=0)


def shards(hidden, w_query, w_key, w_value, key_codes, codebook, positions, cotangent):
    rows, feats = hidden.shape
    width = w_query.shape[0]
    heads = w_query.shape[1] // HD
    levels = codebook.shape[1]
    n_t, n_d = lax.axis_size("tensor"), lax.axis_size("tokens")
    subs, tile = SUBS, rows // SUBS
    cols, total = heads * tile, rows * n_d
    trig = trig_table(positions, HD)
    pos = positions.reshape(1, rows)
    anywhere = pl.BlockSpec(memory_space=pl.ANY)
    vmem = pl.BlockSpec(memory_space=pltpu.VMEM)
    dma = pltpu.SemaphoreType.DMA
    bf16, f32 = jnp.bfloat16, jnp.float32
    out, grad = pl.pallas_call(
        functools.partial(kernel, n_t, n_d, heads),
        out_shape=(
            jax.ShapeDtypeStruct((rows, heads * HD), bf16),
            jax.ShapeDtypeStruct((levels, HD), f32),
        ),
        in_specs=[anywhere] * 6 + [vmem] * 3,
        out_specs=(vmem, vmem),
        scratch_shapes=[
            pltpu.VMEM((subs, n_t, tile, feats), bf16),
            pltpu.VMEM((width, heads * HD + 2 * HD), bf16),
            pltpu.VMEM((rows, heads * HD + 2 * HD), f32),
            pltpu.VMEM((n_d, rows, HD), jnp.int32),
            pltpu.VMEM((n_d, rows, HD), f32),
            pltpu.VMEM((n_d, rows, HD), bf16),
            pltpu.VMEM((n_d, rows, HD), bf16),
            pltpu.VMEM((subs, HD, n_d * tile), bf16),
            pltpu.VMEM((subs, cols, HD), bf16),
            pltpu.VMEM((subs, cols, HD), bf16),
            pltpu.VMEM((subs, HD, cols), f32),
            pltpu.VMEM((subs, n_d, rows, cols), bf16),
            pltpu.VMEM((n_d, rows, cols), f32),
            pltpu.VMEM((subs, 8, cols), f32),
            pltpu.VMEM((levels, 8, HD), f32),
            pltpu.VMEM((n_d, levels, HD), f32),
            pltpu.VMEM((subs, 8, HD), jnp.int32),
            pltpu.VMEM((subs, HD, cols), f32),
            dma((2, subs, n_t)),
            dma((subs, n_t)),
            dma,
            dma((3, n_t)),
            dma((2, n_d)),
            dma((2, n_d)),
            dma((2,)),
            dma((n_d,)),
            dma((n_d,)),
            dma((subs, n_d)),
            dma((subs, n_d)),
            dma((n_d,)),
            dma((n_d,)),
        ],
        compiler_params=pltpu.CompilerParams(
            collective_id=0, has_side_effects=True, vmem_limit_bytes=67043328
        ),
    )(
        hidden.reshape(subs, tile, feats), w_query, w_key, w_value,
        key_codes, trig, codebook.T, pos, cotangent,
    )
    return out, grad.T


def solution(mesh):
    placed = (
        P("tokens", "tensor"),
        P(None, "tensor"),
        P(None, "tensor"),
        P(None, "tensor"),
        P("tokens", "tensor"),
        P("tensor", None),
        P("tokens"),
        P("tokens", "tensor"),
    )
    return jax.shard_map(
        shards,
        mesh=mesh,
        in_specs=placed,
        out_specs=(P("tokens", "tensor"), P("tensor", None)),
        check_vma=False,
    )
```
